32 devices in a mesh: groups: 2 (over y), frame: 4 (over z), head: 2 (over x), seq: 2 (over core).
Axes of the slice: x: 2, y: 2, z: 4, core: 2. Of those that a mesh axis runs over, the one named last changes fastest.
Arguments:
- queries: bfloat16 [32, 1024, 1280], P(('groups', 'frame'), 'seq', 'head'), parts along dimension 0, may hold values from -240 to 240
- key_states: bfloat16 [32, 1024, 1280], P(('groups', 'frame'), 'seq', 'head'), parts along dimension 0, may hold values from -6.5 to 6.5
- value_states: bfloat16 [32, 1024, 1280], P(('groups', 'frame'), 'seq', 'head'), parts along dimension 0, may hold values from -6 to 6
Outputs:
- attended: bfloat16 [32, 1024, 1280], P(('groups', 'frame'), 'seq', 'head'), parts along dimension 0
The draws below stay inside these ranges and needn't reach their ends.
There are 2 independent parts, one for each index of `groups`. The reference program is written for one: setup_inputs(seed, part) draws one part's arguments, and reference() takes and returns one part's arrays. A program takes and returns all parts, laid end to end along the dimension named above; each array names one. Nothing has to cross between parts.
All inputs are finite; a program needn't handle non-finite values.
Results may differ from the reference program's by a relative error of at most 0.0075.
Values may be sent and summed in bfloat16 or wider, within the bound.
A program may use at most 128 MiB of HBM per device.

```python
import jax
import jax.numpy as jnp
from jax import lax

HEAD_DIM = 64
FRAME_TOK = 1024
FRAMES = 16
WIDTH = 1280


def shared_keys(key):
    drawn = jax.random.normal(jax.random.fold_in(key, 7), (FRAMES, FRAME_TOK, WIDTH), jnp.float32)
    return jnp.clip(drawn, -6.0, 6.0)


def draw_key_states(key, part):
    key_values = shared_keys(key)
    return key_values.astype(jnp.bfloat16)


def draw_queries(key, part):
    shape = (FRAMES, FRAME_TOK, WIDTH)
    drawn = jnp.clip(jax.random.normal(jax.random.fold_in(key, 11), shape, jnp.float32), -6.0, 6.0)
    return drawn.astype(jnp.bfloat16)


def steps_of(rng, shape, pieces, low, high):
    factor_of = 1.0
    for position, parts in pieces:
        draws = jax.random.uniform(jax.random.fold_in(jax.random.fold_in(rng, 6), position), (parts,), jnp.float32, low / len(pieces), high / len(pieces))
        factor_of = factor_of * jnp.repeat(jnp.exp(draws), shape[position] // parts).reshape((-1,) + (1,) * (len(shape) - 1 - position))
    return factor_of


def normal_values(rng, shape, scale, bound, cuts=(), kind=jnp.bfloat16):
    result = scale * jax.random.normal(rng, shape, jnp.float32)
    if cuts:
        result = result * steps_of(rng, shape, cuts, -0.22, 0.18)
    return jnp.clip(result, -bound, bound).astype(kind)


def setup_inputs(seed: int = 0, part: int = 0) -> dict:
    arg_keys = jax.random.split(jax.random.key(seed), 4)
    part_splits = jax.random.split(jax.random.fold_in(arg_keys[3], part), 4)
    return {
        "queries": draw_queries(jax.random.fold_in(jax.random.fold_in(arg_keys[3], part), 71), part),
        "key_states": draw_key_states(jax.random.fold_in(jax.random.fold_in(arg_keys[3], part), 71), part),
        "value_states": normal_values(part_splits[2], (FRAMES, FRAME_TOK, WIDTH), 1.0, 6.0, ((0, 4), (1, 2), (2, 2))),
    }


def attend(query_rows, key_rows, value_rows):
    row_count = query_rows.shape[0]
    head_count = query_rows.shape[1] // HEAD_DIM
    query_heads = query_rows.reshape(row_count, head_count, HEAD_DIM).astype(jnp.float32)
    key_heads = key_rows.reshape(key_rows.shape[0], head_count, HEAD_DIM).astype(jnp.float32)
    value_heads = value_rows.reshape(value_rows.shape[0], head_count, HEAD_DIM).astype(jnp.float32)
    scores = jnp.einsum("rhd,khd->hrk", query_heads, key_heads) * (HEAD_DIM ** -0.5)
    row_max = jnp.max(scores, axis=2, keepdims=True)
    weights = jnp.exp(scores - row_max)
    row_sum = jnp.sum(weights, axis=2, keepdims=True)
    rounded = weights.astype(jnp.bfloat16).astype(jnp.float32)
    outputs = jnp.einsum("hrk,khd->hrd", rounded, value_heads) / row_sum
    return outputs.transpose(1, 0, 2).reshape(row_count, head_count * HEAD_DIM).astype(jnp.bfloat16)


def reference(queries, key_states, value_states):
    def one_frame(frame_idx):
        prior_idx = jnp.maximum(frame_idx - 1, 0).astype(jnp.int32)
        key_set = jnp.concatenate([key_states[0], lax.dynamic_index_in_dim(key_states, prior_idx, 0, False)], 0)
        value_set = jnp.concatenate([value_states[0], lax.dynamic_index_in_dim(value_states, prior_idx, 0, False)], 0)
        query_now = lax.dynamic_index_in_dim(queries, frame_idx, 0, False)
        return attend(query_now, key_set, value_set)

    return lax.map(one_frame, jnp.arange(FRAMES, dtype=jnp.int32))
```

```python
import functools

import jax
import jax.numpy as jnp
from jax import lax
from jax.experimental import pallas as pl
from jax.experimental.pallas import tpu as pltpu
from jax.sharding import PartitionSpec as P

HEAD_DIM = 64
LANES = 128
KEY_BLOCK = 512


def attend_columns(q, keys, values):
    rows, width = q.shape
    heads = width // HEAD_DIM
    head_of_lane = lax.broadcasted_iota(jnp.int32, q.shape, 1) // HEAD_DIM
    scaled = q * jnp.asarray(HEAD_DIM**-0.5, q.dtype)
    stacked = jnp.concatenate(
        [jnp.where(head_of_lane == h, scaled, jnp.zeros_like(scaled)) for h in range(heads)], 0
    )
    row_max = total = None
    for k, v in zip(keys, values):
        for start in range(0, k.shape[0], KEY_BLOCK):
            k_part, v_part = k[start : start + KEY_BLOCK], v[start : start + KEY_BLOCK]
            summed = jnp.concatenate([v_part, jnp.ones_like(v_part)], 1)
            scores = lax.dot_general(
                stacked, k_part, (((1,), (1,)), ((), ())), preferred_element_type=jnp.float32
            )
            newer = jnp.max(scores, axis=1, keepdims=True)
            if row_max is not None:
                newer = jnp.maximum(row_max, newer)
            rounded = jnp.exp(scores - newer).astype(jnp.bfloat16)
            part = jnp.dot(rounded, summed, preferred_element_type=jnp.float32)
            total = part if row_max is None else total * jnp.exp(row_max - newer) + part
            row_max = newer
    out = total[:, :width] / total[:, width:]
    result = out[:rows]
    for h in range(1, heads):
        result = jnp.where(head_of_lane == h, out[h * rows : (h + 1) * rows], result)
    return result.astype(jnp.bfloat16)


def kernel(
    blocks,
    halves,
    q_ref,
    k_ref,
    v_ref,
    o_ref,
    k_buf,
    v_buf,
    own_sem,
    swap_send,
    swap_recv,
    prior_send,
    prior_recv,
    anchor_send,
    anchor_recv,
    relay_send,
    relay_recv,
):
    frames, rows, columns = q_ref.shape
    chunks = own_sem.shape[1]
    width = columns // chunks
    anchor_slot, prior_slot = frames, frames + 1
    z = lax.axis_index("frame")
    half = lax.axis_index("seq")
    later = (z + blocks - 1) // blocks
    ahead = {"frame": (z + 1) % blocks}
    first = z == 0
    sends_on = z < blocks - 1
    mine = pl.ds(pl.multiple_of(half * rows, rows), rows)
    sources, buffers = (k_ref, v_ref), (k_buf, v_buf)
    offsets = range(1, halves)

    def cols(c):
        return pl.ds(pl.multiple_of(c * width, LANES), width) if chunks > 1 else pl.ds(0, width)

    def sibling(j):
        return {"seq": (half + j) % halves}

    def remote(src, dst, send, recv, where):
        return pltpu.make_async_remote_copy(
            src_ref=src,
            dst_ref=dst,
            send_sem=send,
            recv_sem=recv,
            device_id=where,
            device_id_type=pl.DeviceIdType.MESH,
        )

    def own(i, c):
        return pltpu.make_async_copy(
            sources[i].at[pl.ds(0, frames - 1), :, cols(c)],
            buffers[i].at[pl.ds(0, frames - 1), mine, cols(c)],
            own_sem.at[i, c],
        )

    def swap(i, c, j):
        return remote(
            sources[i].at[pl.ds(0, frames - 1), :, cols(c)],
            buffers[i].at[pl.ds(0, frames - 1), mine, cols(c)],
            swap_send.at[i, c, j - 1],
            swap_recv.at[i, c, j - 1],
            sibling(j),
        )

    def prior(i, c):
        return remote(
            sources[i].at[frames - 1, :, cols(c)],
            buffers[i].at[prior_slot, mine, cols(c)],
            prior_send.at[i, c],
            prior_recv.at[i, c],
            ahead,
        )

    def anchor(i, c, root):
        here = buffers[i].at[anchor_slot, mine, cols(c)]
        return remote(
            sources[i].at[0, :, cols(c)] if root else here,
            here,
            anchor_send.at[i, c],
            anchor_recv.at[i, c],
            ahead,
        )

    def relay(which, i, c, j):
        here = buffers[i].at[anchor_slot + which, mine, cols(c)]
        return remote(
            here,
            here,
            relay_send.at[which, i, c, j - 1],
            relay_recv.at[which, i, c, j - 1],
            sibling(j),
        )

    barrier = pltpu.get_barrier_semaphore()

    @pl.when(sends_on)
    def _():
        pl.semaphore_signal(
            barrier, inc=1, device_id=ahead, device_id_type=pl.DeviceIdType.MESH
        )

    @pl.when(z > 0)
    def _():
        pl.semaphore_signal(
            barrier,
            inc=1,
            device_id={"frame": (z + blocks - 1) % blocks},
            device_id_type=pl.DeviceIdType.MESH,
        )

    for j in offsets:
        pl.semaphore_signal(
            barrier, inc=1, device_id=sibling(j), device_id_type=pl.DeviceIdType.MESH
        )
    pl.semaphore_wait(barrier, later + 1 - (z + 1) // blocks + halves - 1)

    @pl.when(first & sends_on)
    def _():
        @pl.loop(0, chunks)
        def _(c):
            for i in range(2):
                anchor(i, c, True).start()
            for i in range(2):
                prior(i, c).start()

    @pl.when((z > 0) & sends_on)
    def _():
        for i in range(2):
            prior(i, 0).start()

    @pl.loop(0, chunks)
    def _(c):
        for i in range(2):
            own(i, c).start()
            for j in offsets:
                swap(i, c, j).start()

    def receive(c):
        @pl.when(z > 0)
        def _():
            for i in range(2):
                anchor(i, c, False).wait_recv()

                @pl.when(sends_on)
                def _():
                    anchor(i, c, False).start()

                for j in offsets:
                    relay(0, i, c, j).start()

            @pl.when(sends_on & (c + 1 < chunks))
            def _():
                for i in range(2):
                    prior(i, c + 1).start()

            for i in range(2):
                prior(i, c).wait_recv()
                for j in offsets:
                    relay(1, i, c, j).start()

    def complete(c):
        for i in range(2):
            own(i, c).wait()
            for j in offsets:
                swap(i, c, j).wait_recv()

        @pl.when(z > 0)
        def _():
            for i in range(2):
                for j in offsets:
                    relay(0, i, c, j).wait_recv()
                    relay(1, i, c, j).wait_recv()

    block = min(rows, 512)
    per_frame = rows // block
    steps = frames * per_frame

    def compute(c, step):
        frame = step // per_frame
        opens = (frames - frame) // frames
        before = (frame - 1) * (1 - opens) + opens * later * prior_slot
        zero = later * anchor_slot
        at_rows = pl.ds(pl.multiple_of((step % per_frame) * block, block), block)
        for start in range(0, width, LANES):
            size = min(LANES, width - start)
            if chunks > 1:
                at = cols(c)
            else:
                at = pl.ds(start, size)
            o_ref[frame, at_rows, at] = attend_columns(
                q_ref[frame, at_rows, at],
                [k_buf[zero, :, at], k_buf[before, :, at]],
                [v_buf[zero, :, at], v_buf[before, :, at]],
            )

    receive(0)

    @pl.loop(0, chunks)
    def _(c):
        complete(c)

        @pl.loop(0, steps)
        def _(step):
            @pl.when((step == steps // 2) & (c + 1 < chunks))
            def _():
                receive(c + 1)

            compute(c, step)

    @pl.loop(0, chunks)
    def _(c):
        for i in range(2):
            for j in offsets:
                swap(i, c, j).wait_send()

            @pl.when(sends_on)
            def _():
                prior(i, c).wait_send()
                anchor(i, c, False).wait_send()

            @pl.when(z > 0)
            def _():
                for j in offsets:
                    relay(0, i, c, j).wait_send()
                    relay(1, i, c, j).wait_send()


def local(blocks, halves, queries, key_states, value_states):
    frames, rows, columns = queries.shape
    chunks = columns // LANES if columns % LANES == 0 else 1
    held = pltpu.VMEM((frames + 2, rows * halves, columns), queries.dtype)
    dma = pltpu.SemaphoreType.DMA
    plain = dma((2, chunks))
    across = dma((2, chunks, halves - 1))
    relays = dma((2, 2, chunks, halves - 1))
    anywhere = pl.BlockSpec(memory_space=pl.ANY)
    near = pl.BlockSpec(memory_space=pltpu.VMEM)
    return pl.pallas_call(
        functools.partial(kernel, blocks, halves),
        out_shape=jax.ShapeDtypeStruct(queries.shape, queries.dtype),
        in_specs=[near, anywhere, anywhere],
        out_specs=near,
        scratch_shapes=[
            held,
            held,
            plain,
            across,
            across,
            plain,
            plain,
            plain,
            plain,
            relays,
            relays,
        ],
        compiler_params=pltpu.CompilerParams(
            collective_id=0, has_side_effects=True, vmem_limit_bytes=56 * 1024 * 1024
        ),
    )(queries, key_states, value_states)


SLOT_KEYS = 256
ONES_ROWS = 16
BF = jnp.bfloat16
F32 = jnp.float32
NT = (((1,), (1,)), ((), ()))
LOG2E = 1.4426950408889634


def parts_of(q):
    scaled = q.astype(F32) * (LOG2E * HEAD_DIM**-0.5)
    high = scaled.astype(BF)
    return high, (scaled - high.astype(F32)).astype(BF)


def shifted_kernel(
    blocks,
    q_ref,
    k_ref,
    v_ref,
    o_ref,
    k_buf,
    v_buf,
    q_next,
    o_next,
    o_first,
    vt,
    parts,
    s0,
    s1,
    p0,
    p1,
    m0,
    m1,
    flat,
    flat_b,
    own_sem,
    swap_send,
    swap_recv,
    anchor_send,
    anchor_recv,
    relay_send,
    relay_recv,
    q_send,
    q_recv,
    o_send,
    o_recv,
):
    frames, rows, columns = q_ref.shape
    chunks = columns // LANES
    tokens = k_buf.shape[1]
    z = lax.axis_index("frame")
    half = lax.axis_index("seq")
    later = (z + blocks - 1) // blocks
    last = (z + 1) // blocks
    ahead = {"frame": (z + 1) % blocks}
    behind = {"frame": (z + blocks - 1) % blocks}
    sibling = {"seq": 1 - half}
    first = z == 0
    sends_on = z < blocks - 1
    mine = pl.ds(pl.multiple_of(half * rows, rows), rows)
    sources, buffers = (k_ref, v_ref), (k_buf, v_buf)
    anchor_slot = frames
    zero_slot = later * anchor_slot

    def cols(c):
        return pl.ds(pl.multiple_of(c * LANES, LANES), LANES)

    def remote(src, dst, send, recv, where):
        return pltpu.make_async_remote_copy(
            src_ref=src,
            dst_ref=dst,
            send_sem=send,
            recv_sem=recv,
            device_id=where,
            device_id_type=pl.DeviceIdType.MESH,
        )

    def own(i, c):
        return pltpu.make_async_copy(
            sources[i].at[:, :, cols(c)],
            buffers[i].at[pl.ds(0, frames), mine, cols(c)],
            own_sem.at[i, c],
        )

    def swap(i, c):
        return remote(
            sources[i].at[:, :, cols(c)],
            buffers[i].at[pl.ds(0, frames), mine, cols(c)],
            swap_send.at[i, c],
            swap_recv.at[i, c],
            sibling,
        )

    def anchor(i, c, root):
        here = buffers[i].at[anchor_slot, mine, cols(c)]
        return remote(
            sources[i].at[0, :, cols(c)] if root else here,
            here,
            anchor_send.at[i, c],
            anchor_recv.at[i, c],
            ahead,
        )

    def relay(i, c):
        here = buffers[i].at[anchor_slot, mine, cols(c)]
        return remote(here, here, relay_send.at[i, c], relay_recv.at[i, c], sibling)

    def lend(c):
        return remote(
            q_ref.at[0, :, cols(c)], q_next.at[:, cols(c)], q_send.at[c], q_recv.at[c], behind
        )

    def give(c):
        return remote(
            o_next.at[:, cols(c)], o_first.at[:, cols(c)], o_send.at[c], o_recv.at[c], ahead
        )

    barrier = pltpu.get_barrier_semaphore()

    def greet(where):
        pl.semaphore_signal(barrier, inc=1, device_id=where, device_id_type=pl.DeviceIdType.MESH)

    @pl.when(sends_on)
    def _():
        greet(ahead)

    @pl.when(z > 0)
    def _():
        greet(behind)

    greet(sibling)
    pl.semaphore_wait(barrier, later + 1 - last + 1)

    @pl.loop(0, chunks)
    def _(c):
        @pl.when(first & sends_on)
        def _():
            for i in range(2):
                anchor(i, c, True).start()

        for i in range(2):
            own(i, c).start()
            swap(i, c).start()

        @pl.when(z > 0)
        def _():
            lend(c).start()

    vt[:, :, :, HEAD_DIM:, :] = jnp.ones((*vt.shape[:3], ONES_ROWS, tokens), BF)

    def receive(c):
        @pl.when(z > 0)
        def _():
            for i in range(2):
                anchor(i, c, False).wait_recv()

                @pl.when(sends_on)
                def _():
                    anchor(i, c, False).start()

                relay(i, c).start()

    low_lanes = lax.broadcasted_iota(jnp.int32, (SLOT_KEYS, LANES), 1) < HEAD_DIM

    def prepare(c, par):
        for i in range(2):
            own(i, c).wait()
            swap(i, c).wait_recv()

        @pl.when(z > 0)
        def _():
            for i in range(2):
                relay(i, c).wait_recv()

        @pl.when(sends_on)
        def _():
            lend(c).wait_recv()

        @pl.loop(0, frames + later * (1 - last))
        def _(n):
            slot = n + last * (n // (frames - 1))

            @pl.loop(0, tokens // SLOT_KEYS)
            def _(b):
                at = pl.ds(pl.multiple_of(b * SLOT_KEYS, SLOT_KEYS), SLOT_KEYS)
                v = v_buf[slot, at, cols(c)].T
                vt[par, slot, 0, 0:HEAD_DIM, at] = v[:HEAD_DIM]
                vt[par, slot, 1, 0:HEAD_DIM, at] = v[HEAD_DIM:]

        def put_q(n, q, at):
            for t, part in enumerate(parts_of(q)):
                lanes = pl.ds(t * LANES, LANES)
                none = jnp.zeros_like(part)
                parts[par, n, 0, at, lanes] = jnp.where(low_lanes, part, none)
                parts[par, n, 1, at, lanes] = jnp.where(low_lanes, none, part)

        @pl.loop(0, rows // SLOT_KEYS)
        def _(b):
            at = pl.ds(pl.multiple_of(b * SLOT_KEYS, SLOT_KEYS), SLOT_KEYS)

            @pl.loop(0, frames)
            def _(n):
                put_q(n, q_ref[n, at, cols(c)], at)

            @pl.when(sends_on)
            def _():
                put_q(frames, q_next[at, cols(c)], at)

    tasks = frames - last
    units = 2 * tasks

    def task_of(t):
        lent = (1 - last) * ((t + 2) // frames) * (1 - (t + 1) // frames)
        final = (t + 1) // tasks
        number = lent * frames + (1 - lent) * (final * (frames - 1) + (1 - final) * (t + 1))
        return number, lent

    def split(u):
        c = u // units
        return c, c % 2, (u % units) // 2

    def phase(u, head, a, b, cc):
        if b is not None:
            s_ref, m_ref, p_ref = b
            _, _, t = split(u + 1)
            joint = jnp.where(first & (t == 0), 0.0, 1.0).astype(F32)
            ma = jnp.max(m_ref[0], axis=0, keepdims=True)
            mb = jnp.max(m_ref[1], axis=0, keepdims=True)
            both = jnp.maximum(ma, mb)
            tops = [jnp.where(joint > 0.5, both, x) for x in (ma, mb)]
            for n in range(2):
                for k0 in range(n * tokens, (n + 1) * tokens, SLOT_KEYS):
                    at = slice(k0, k0 + SLOT_KEYS)
                    p_ref[at, :] = jnp.exp2(s_ref[at, :] - tops[n]).astype(BF)
        if cc is not None:
            (p_ref,) = cc
            c, par, t = split(u)
            number, lent = task_of(t)
            part_a = jnp.dot(
                vt[par, zero_slot, head], p_ref[:tokens, :], preferred_element_type=F32
            )
            part_b = jnp.dot(
                vt[par, number - 1, head], p_ref[tokens:, :], preferred_element_type=F32
            )
            alone = first & (t == 0)
            total = jnp.where(jnp.where(alone, 1, 0) > 0, part_a, part_a + part_b)
            mine_rows = slice(head * HEAD_DIM, (head + 1) * HEAD_DIM)
            flat[mine_rows, :] = total[:HEAD_DIM] / total[HEAD_DIM : HEAD_DIM + 1]
            flat_b[mine_rows, :] = part_b[:HEAD_DIM] / part_b[HEAD_DIM : HEAD_DIM + 1]
        if a is not None:
            s_ref, m_ref = a
            c, par, t = split(u + 2)
            number, _ = task_of(t)
            alone = jnp.where(first & (t == 0), 1, 0)
            places = ((zero_slot, number - alone), (number - 1, number))
            for n, (slot, frame) in enumerate(places):
                q = parts[par, frame, head]
                top = None
                for k0 in range(0, tokens, SLOT_KEYS):
                    k = k_buf[slot, k0 : k0 + SLOT_KEYS, cols(c)]
                    scores = lax.dot_general(
                        jnp.concatenate([k, k], 1), q, NT, preferred_element_type=F32
                    )
                    s_ref[n * tokens + k0 : n * tokens + k0 + SLOT_KEYS, :] = scores
                    newer = jnp.max(scores.reshape(SLOT_KEYS // 8, 8, rows), axis=0)
                    top = newer if top is None else jnp.maximum(top, newer)
                m_ref[n] = top

    def finish(u):
        c, _, t = split(u)
        number, lent = task_of(t)

        @pl.when(lent == 0)
        def _():
            o_ref[number, :, cols(c)] = flat[...].T.astype(BF)

        @pl.when(first & (t == 0))
        def _():
            o_ref[0, :, cols(c)] = flat[...].T.astype(BF)
            o_ref[1, :, cols(c)] = flat_b[...].T.astype(BF)

        @pl.when(lent == 1)
        def _():
            o_next[:, cols(c)] = flat[...].T.astype(BF)
            give(c).start()

    count = chunks * units
    receive(0)
    prepare(0, 0)
    phase(-2, 0, (s0, m0), None, None)
    phase(-1, 1, (s1, m1), (s0, m0, p0), None)

    @pl.loop(0, count - 2)
    def _(u):
        c = u // units
        step = u % units

        @pl.when((step == units - 6) & (c + 1 < chunks))
        def _():
            receive(c + 1)

        @pl.when((step == units - 2) & (c + 1 < chunks))
        def _():
            prepare(c + 1, (c + 1) % 2)

        @pl.when(u % 2 == 0)
        def _():
            phase(u, 0, (s0, m0), (s1, m1, p1), (p0,))

        @pl.when(u % 2 == 1)
        def _():
            phase(u, 1, (s1, m1), (s0, m0, p0), (p1,))
            finish(u)

    phase(count - 2, 0, None, (s1, m1, p1), (p0,))
    phase(count - 1, 1, None, None, (p1,))
    finish(count - 1)

    @pl.loop(0, chunks)
    def _(c):
        for i in range(2):
            swap(i, c).wait_send()

            @pl.when(sends_on)
            def _():
                anchor(i, c, False).wait_send()

            @pl.when(z > 0)
            def _():
                relay(i, c).wait_send()

        @pl.when(sends_on)
        def _():
            give(c).wait_send()

        @pl.when(z > 0)
        def _():
            lend(c).wait_send()
            give(c).wait_recv()
            o_ref[0, :, cols(c)] = o_first[:, cols(c)]


def shifted(blocks, queries, key_states, value_states):
    frames, rows, columns = queries.shape
    tokens = 2 * rows
    chunks = columns // LANES
    held = pltpu.VMEM((frames + 1, tokens, columns), BF)
    flat = pltpu.VMEM((rows, columns), BF)
    dma = pltpu.SemaphoreType.DMA
    pair, single = dma((2, chunks)), dma((chunks,))
    anywhere = pl.BlockSpec(memory_space=pl.ANY)
    near = pl.BlockSpec(memory_space=pltpu.VMEM)
    scores = pltpu.VMEM((2 * tokens, rows), F32)
    weights = pltpu.VMEM((2 * tokens, rows), BF)
    tops = pltpu.VMEM((2, 8, rows), F32)
    turned_out = pltpu.VMEM((LANES, rows), F32)
    return pl.pallas_call(
        functools.partial(shifted_kernel, blocks),
        out_shape=jax.ShapeDtypeStruct(queries.shape, queries.dtype),
        in_specs=[near, anywhere, anywhere],
        out_specs=near,
        scratch_shapes=[
            held,
            held,
            flat,
            flat,
            flat,
            pltpu.VMEM((2, frames + 1, 2, HEAD_DIM + ONES_ROWS, tokens), BF),
            pltpu.VMEM((2, frames + 1, 2, rows, 2 * LANES), BF),
            scores,
            scores,
            weights,
            weights,
            tops,
            tops,
            turned_out,
            turned_out,
            *[pair] * 7,
            *[single] * 4,
        ],
        compiler_params=pltpu.CompilerParams(
            collective_id=0, has_side_effects=True, vmem_limit_bytes=58 * 1024 * 1024
        ),
    )(queries, key_states, value_states)


def solution(mesh):
    spec = P(("groups", "frame"), "seq", "head")
    blocks, halves = mesh.shape["frame"], mesh.shape["seq"]

    def body(queries, key_states, value_states):
        frames, rows, columns = queries.shape
        fits = columns % LANES == 0 and rows % SLOT_KEYS == 0
        if blocks > 1 and halves == 2 and frames >= 4 and fits:
            return shifted(blocks, queries, key_states, value_states)
        return local(blocks, halves, queries, key_states, value_states)

    return jax.shard_map(
        body, mesh=mesh, in_specs=(spec, spec, spec), out_specs=spec, check_vma=False
    )
```

```python
import functools

import jax
import jax.numpy as jnp
from jax import lax
from jax.experimental import pallas as pl
from jax.experimental.pallas import tpu as pltpu
from jax.sharding import PartitionSpec as P

HEAD_DIM = 64
LANES = 128
KEY_BLOCK = 512


def attend_columns(q, keys, values):
    rows, width = q.shape
    heads = width // HEAD_DIM
    head_of_lane = lax.broadcasted_iota(jnp.int32, q.shape, 1) // HEAD_DIM
    scaled = q * jnp.asarray(HEAD_DIM**-0.5, q.dtype)
    stacked = jnp.concatenate(
        [jnp.where(head_of_lane == h, scaled, jnp.zeros_like(scaled)) for h in range(heads)], 0
    )
    row_max = total = None
    for k, v in zip(keys, values):
        for start in range(0, k.shape[0], KEY_BLOCK):
            k_part, v_part = k[start : start + KEY_BLOCK], v[start : start + KEY_BLOCK]
            summed = jnp.concatenate([v_part, jnp.ones_like(v_part)], 1)
            scores = lax.dot_general(
                stacked, k_part, (((1,), (1,)), ((), ())), preferred_element_type=jnp.float32
            )
            newer = jnp.max(scores, axis=1, keepdims=True)
            if row_max is not None:
                newer = jnp.maximum(row_max, newer)
            rounded = jnp.exp(scores - newer).astype(jnp.bfloat16)
            part = jnp.dot(rounded, summed, preferred_element_type=jnp.float32)
            total = part if row_max is None else total * jnp.exp(row_max - newer) + part
            row_max = newer
    out = total[:, :width] / total[:, width:]
    result = out[:rows]
    for h in range(1, heads):
        result = jnp.where(head_of_lane == h, out[h * rows : (h + 1) * rows], result)
    return result.astype(jnp.bfloat16)


def kernel(
    blocks,
    halves,
    q_ref,
    k_ref,
    v_ref,
    o_ref,
    k_buf,
    v_buf,
    own_sem,
    swap_send,
    swap_recv,
    prior_send,
    prior_recv,
    anchor_send,
    anchor_recv,
    relay_send,
    relay_recv,
):
    frames, rows, columns = q_ref.shape
    chunks = own_sem.shape[1]
    width = columns // chunks
    anchor_slot, prior_slot = frames, frames + 1
    z = lax.axis_index("frame")
    half = lax.axis_index("seq")
    later = (z + blocks - 1) // blocks
    ahead = {"frame": (z + 1) % blocks}
    first = z == 0
    sends_on = z < blocks - 1
    mine = pl.ds(pl.multiple_of(half * rows, rows), rows)
    sources, buffers = (k_ref, v_ref), (k_buf, v_buf)
    offsets = range(1, halves)

    def cols(c):
        return pl.ds(pl.multiple_of(c * width, LANES), width) if chunks > 1 else pl.ds(0, width)

    def sibling(j):
        return {"seq": (half + j) % halves}

    def remote(src, dst, send, recv, where):
        return pltpu.make_async_remote_copy(
            src_ref=src,
            dst_ref=dst,
            send_sem=send,
            recv_sem=recv,
            device_id=where,
            device_id_type=pl.DeviceIdType.MESH,
        )

    def own(i, c):
        return pltpu.make_async_copy(
            sources[i].at[pl.ds(0, frames - 1), :, cols(c)],
            buffers[i].at[pl.ds(0, frames - 1), mine, cols(c)],
            own_sem.at[i, c],
        )

    def swap(i, c, j):
        return remote(
            sources[i].at[pl.ds(0, frames - 1), :, cols(c)],
            buffers[i].at[pl.ds(0, frames - 1), mine, cols(c)],
            swap_send.at[i, c, j - 1],
            swap_recv.at[i, c, j - 1],
            sibling(j),
        )

    def prior(i, c):
        return remote(
            sources[i].at[frames - 1, :, cols(c)],
            buffers[i].at[prior_slot, mine, cols(c)],
            prior_send.at[i, c],
            prior_recv.at[i, c],
            ahead,
        )

    def anchor(i, c, root):
        here = buffers[i].at[anchor_slot, mine, cols(c)]
        return remote(
            sources[i].at[0, :, cols(c)] if root else here,
            here,
            anchor_send.at[i, c],
            anchor_recv.at[i, c],
            ahead,
        )

    def relay(which, i, c, j):
        here = buffers[i].at[anchor_slot + which, mine, cols(c)]
        return remote(
            here,
            here,
            relay_send.at[which, i, c, j - 1],
            relay_recv.at[which, i, c, j - 1],
            sibling(j),
        )

    barrier = pltpu.get_barrier_semaphore()

    @pl.when(sends_on)
    def _():
        pl.semaphore_signal(
            barrier, inc=1, device_id=ahead, device_id_type=pl.DeviceIdType.MESH
        )

    @pl.when(z > 0)
    def _():
        pl.semaphore_signal(
            barrier,
            inc=1,
            device_id={"frame": (z + blocks - 1) % blocks},
            device_id_type=pl.DeviceIdType.MESH,
        )

    for j in offsets:
        pl.semaphore_signal(
            barrier, inc=1, device_id=sibling(j), device_id_type=pl.DeviceIdType.MESH
        )
    pl.semaphore_wait(barrier, later + 1 - (z + 1) // blocks + halves - 1)

    @pl.when(first & sends_on)
    def _():
        @pl.loop(0, chunks)
        def _(c):
            for i in range(2):
                anchor(i, c, True).start()
            for i in range(2):
                prior(i, c).start()

    @pl.when((z > 0) & sends_on)
    def _():
        for i in range(2):
            prior(i, 0).start()

    @pl.loop(0, chunks)
    def _(c):
        for i in range(2):
            own(i, c).start()
            for j in offsets:
                swap(i, c, j).start()

    def receive(c):
        @pl.when(z > 0)
        def _():
            for i in range(2):
                anchor(i, c, False).wait_recv()

                @pl.when(sends_on)
                def _():
                    anchor(i, c, False).start()

                for j in offsets:
                    relay(0, i, c, j).start()

            @pl.when(sends_on & (c + 1 < chunks))
            def _():
                for i in range(2):
                    prior(i, c + 1).start()

            for i in range(2):
                prior(i, c).wait_recv()
                for j in offsets:
                    relay(1, i, c, j).start()

    def complete(c):
        for i in range(2):
            own(i, c).wait()
            for j in offsets:
                swap(i, c, j).wait_recv()

        @pl.when(z > 0)
        def _():
            for i in range(2):
                for j in offsets:
                    relay(0, i, c, j).wait_recv()
                    relay(1, i, c, j).wait_recv()

    block = min(rows, 512)
    per_frame = rows // block
    steps = frames * per_frame

    def compute(c, step):
        frame = step // per_frame
        opens = (frames - frame) // frames
        before = (frame - 1) * (1 - opens) + opens * later * prior_slot
        zero = later * anchor_slot
        at_rows = pl.ds(pl.multiple_of((step % per_frame) * block, block), block)
        for start in range(0, width, LANES):
            size = min(LANES, width - start)
            if chunks > 1:
                at = cols(c)
            else:
                at = pl.ds(start, size)
            o_ref[frame, at_rows, at] = attend_columns(
                q_ref[frame, at_rows, at],
                [k_buf[zero, :, at], k_buf[before, :, at]],
                [v_buf[zero, :, at], v_buf[before, :, at]],
            )

    receive(0)

    @pl.loop(0, chunks)
    def _(c):
        complete(c)

        @pl.loop(0, steps)
        def _(step):
            @pl.when((step == steps // 2) & (c + 1 < chunks))
            def _():
                receive(c + 1)

            compute(c, step)

    @pl.loop(0, chunks)
    def _(c):
        for i in range(2):
            for j in offsets:
                swap(i, c, j).wait_send()

            @pl.when(sends_on)
            def _():
                prior(i, c).wait_send()
                anchor(i, c, False).wait_send()

            @pl.when(z > 0)
            def _():
                for j in offsets:
                    relay(0, i, c, j).wait_send()
                    relay(1, i, c, j).wait_send()


def local(blocks, halves, queries, key_states, value_states):
    frames, rows, columns = queries.shape
    chunks = columns // LANES if columns % LANES == 0 else 1
    held = pltpu.VMEM((frames + 2, rows * halves, columns), queries.dtype)
    dma = pltpu.SemaphoreType.DMA
    plain = dma((2, chunks))
    across = dma((2, chunks, halves - 1))
    relays = dma((2, 2, chunks, halves - 1))
    anywhere = pl.BlockSpec(memory_space=pl.ANY)
    near = pl.BlockSpec(memory_space=pltpu.VMEM)
    return pl.pallas_call(
        functools.partial(kernel, blocks, halves),
        out_shape=jax.ShapeDtypeStruct(queries.shape, queries.dtype),
        in_specs=[near, anywhere, anywhere],
        out_specs=near,
        scratch_shapes=[
            held,
            held,
            plain,
            across,
            across,
            plain,
            plain,
            plain,
            plain,
            relays,
            relays,
        ],
        compiler_params=pltpu.CompilerParams(
            collective_id=0, has_side_effects=True, vmem_limit_bytes=56 * 1024 * 1024
        ),
    )(queries, key_states, value_states)


SLOT_KEYS = 256
ONES_ROWS = 16
ARRIVAL_UNITS = 5
BF = jnp.bfloat16
F32 = jnp.float32
NT = (((1,), (1,)), ((), ()))
LOG2E = 1.4426950408889634


def parts_of(q):
    scaled = q.astype(F32) * (LOG2E * HEAD_DIM**-0.5)
    high = scaled.astype(BF)
    return high, (scaled - high.astype(F32)).astype(BF)


def shifted_kernel(
    blocks,
    q_ref,
    k_ref,
    v_ref,
    o_ref,
    k_buf,
    v_buf,
    q_next,
    o_next,
    o_first,
    vt,
    parts,
    s0,
    s1,
    p0,
    p1,
    m0,
    m1,
    flat,
    flat_b,
    own_sem,
    swap_send,
    swap_recv,
    anchor_send,
    anchor_recv,
    relay_send,
    relay_recv,
    q_send,
    q_recv,
    o_send,
    o_recv,
):
    frames, rows, columns = q_ref.shape
    chunks = columns // LANES
    tokens = k_buf.shape[1]
    z = lax.axis_index("frame")
    half = lax.axis_index("seq")
    later = (z + blocks - 1) // blocks
    last = (z + 1) // blocks
    ahead = {"frame": (z + 1) % blocks}
    behind = {"frame": (z + blocks - 1) % blocks}
    sibling = {"seq": 1 - half}
    first = z == 0
    sends_on = z < blocks - 1
    mine = pl.ds(pl.multiple_of(half * rows, rows), rows)
    sources, buffers = (k_ref, v_ref), (k_buf, v_buf)
    anchor_slot = frames
    zero_slot = later * anchor_slot

    def cols(c):
        return pl.ds(pl.multiple_of(c * LANES, LANES), LANES)

    def remote(src, dst, send, recv, where):
        return pltpu.make_async_remote_copy(
            src_ref=src,
            dst_ref=dst,
            send_sem=send,
            recv_sem=recv,
            device_id=where,
            device_id_type=pl.DeviceIdType.MESH,
        )

    def own(i, c):
        return pltpu.make_async_copy(
            sources[i].at[:, :, cols(c)],
            buffers[i].at[pl.ds(0, frames), mine, cols(c)],
            own_sem.at[i, c],
        )

    def swap(i, c):
        return remote(
            sources[i].at[:, :, cols(c)],
            buffers[i].at[pl.ds(0, frames), mine, cols(c)],
            swap_send.at[i, c],
            swap_recv.at[i, c],
            sibling,
        )

    def anchor(i, c, root):
        here = buffers[i].at[anchor_slot, mine, cols(c)]
        return remote(
            sources[i].at[0, :, cols(c)] if root else here,
            here,
            anchor_send.at[i, c],
            anchor_recv.at[i, c],
            ahead,
        )

    def relay(i, c):
        here = buffers[i].at[anchor_slot, mine, cols(c)]
        return remote(here, here, relay_send.at[i, c], relay_recv.at[i, c], sibling)

    def lend(c):
        return remote(
            q_ref.at[0, :, cols(c)], q_next.at[:, cols(c)], q_send.at[c], q_recv.at[c], behind
        )

    def give(c):
        return remote(
            o_next.at[:, cols(c)], o_first.at[:, cols(c)], o_send.at[c], o_recv.at[c], ahead
        )

    barrier = pltpu.get_barrier_semaphore()

    def greet(where):
        pl.semaphore_signal(barrier, inc=1, device_id=where, device_id_type=pl.DeviceIdType.MESH)

    @pl.when(sends_on)
    def _():
        greet(ahead)

    @pl.when(z > 0)
    def _():
        greet(behind)

    greet(sibling)
    pl.semaphore_wait(barrier, later + 1 - last + 1)

    def begin(c):
        for i in range(2):
            @pl.when(first & sends_on)
            def _():
                anchor(i, c, True).start()

            swap(i, c).start()
            own(i, c).start()
            if i == 0:
                @pl.when(z > 0)
                def _():
                    lend(c).start()

    begin(0)
    vt[:, :, :, HEAD_DIM:, :] = jnp.ones((*vt.shape[:3], ONES_ROWS, tokens), BF)

    def receive(c):
        @pl.when(z > 0)
        def _():
            for i in range(2):
                anchor(i, c, False).wait_recv()

                @pl.when(sends_on)
                def _():
                    anchor(i, c, False).start()

                relay(i, c).start()

    low_lanes = lax.broadcasted_iota(jnp.int32, (SLOT_KEYS, LANES), 1) < HEAD_DIM

    def landed(i, c):
        own(i, c).wait()
        swap(i, c).wait_recv()

        @pl.when(z > 0)
        def _():
            relay(i, c).wait_recv()

    def put_queries(c, n, q, at):
        for t, part in enumerate(parts_of(q)):
            lanes = pl.ds(t * LANES, LANES)
            none = jnp.zeros_like(part)
            parts[c, n, 0, at, lanes] = jnp.where(low_lanes, part, none)
            parts[c, n, 1, at, lanes] = jnp.where(low_lanes, none, part)

    def row_blocks(body):
        @pl.loop(0, rows // SLOT_KEYS)
        def _(b):
            body(pl.ds(pl.multiple_of(b * SLOT_KEYS, SLOT_KEYS), SLOT_KEYS))

    def prepare_keys(c):
        landed(0, c)

        @pl.when(sends_on)
        def _():
            lend(c).wait_recv()
            row_blocks(lambda at: put_queries(c, frames, q_next[at, cols(c)], at))

    def prepare_values(c):
        par = c % 2
        landed(1, c)

        @pl.loop(0, frames + later * (1 - last))
        def _(n):
            slot = n + last * (n // (frames - 1))

            @pl.loop(0, tokens // rows)
            def _(b):
                at = pl.ds(pl.multiple_of(b * rows, rows), rows)
                v = v_buf[slot, at, cols(c)].T
                vt[par, slot, 0, 0:HEAD_DIM, at] = v[:HEAD_DIM]
                vt[par, slot, 1, 0:HEAD_DIM, at] = v[HEAD_DIM:]

    tasks = frames - last
    units = 2 * tasks

    def flag(x):
        return jnp.where(x, 1, 0)

    def task_of(t):
        lent = (1 - last) * flag(t == frames - 2)
        final = flag(t == tasks - 1)
        return lent * frames + (1 - lent) * (t + 1 + final * (frames - 2 - t)), lent

    def split(u):
        c = sum(flag(u >= n * units) for n in range(1, chunks))
        return c, c % 2, (u - c * units) // 2

    def phase(u, head, a, b, cc):
        if b is not None:
            s_ref, m_ref, p_ref = b
            _, _, t = split(u + 1)
            joint = jnp.where(first & (t == 0), 0.0, 1.0).astype(F32)
            ma = jnp.max(m_ref[0], axis=0, keepdims=True)
            mb = jnp.max(m_ref[1], axis=0, keepdims=True)
            both = jnp.maximum(ma, mb)
            tops = [jnp.where(joint > 0.5, both, x) for x in (ma, mb)]
            for n in range(2):
                for k0 in range(n * tokens, (n + 1) * tokens, SLOT_KEYS):
                    at = slice(k0, k0 + SLOT_KEYS)
                    p_ref[at, :] = jnp.exp2(s_ref[at, :] - tops[n]).astype(BF)
        if cc is not None:
            (p_ref,) = cc
            c, par, t = split(u)
            number, lent = task_of(t)
            part_a = jnp.dot(
                vt[par, zero_slot, head], p_ref[:tokens, :], preferred_element_type=F32
            )
            part_b = jnp.dot(
                vt[par, number - 1, head], p_ref[tokens:, :], preferred_element_type=F32
            )
            alone = first & (t == 0)
            total = part_a + jnp.where(flag(alone) > 0, jnp.zeros_like(part_b), part_b)
            mine_rows = slice(head * HEAD_DIM, (head + 1) * HEAD_DIM)
            one = 1.0 / total[HEAD_DIM : HEAD_DIM + 1]
            flat[mine_rows, :] = (total[:HEAD_DIM] * one).astype(BF)
            one = 1.0 / part_b[HEAD_DIM : HEAD_DIM + 1]
            flat_b[mine_rows, :] = (part_b[:HEAD_DIM] * one).astype(BF)
        if a is not None:
            s_ref, m_ref = a
            c, _, t = split(u + 2)
            number, _ = task_of(t)
            alone = jnp.where(first & (t == 0), 1, 0)
            places = ((zero_slot, number - alone), (number - 1, number))
            for n, (slot, frame) in enumerate(places):
                q = parts[c, frame, head]
                top = None
                for k0 in range(0, tokens, SLOT_KEYS):
                    k = k_buf[slot, k0 : k0 + SLOT_KEYS, cols(c)]
                    scores = lax.dot_general(
                        jnp.concatenate([k, k], 1), q, NT, preferred_element_type=F32
                    )
                    s_ref[n * tokens + k0 : n * tokens + k0 + SLOT_KEYS, :] = scores
                    newer = jnp.max(scores.reshape(SLOT_KEYS // 8, 8, rows), axis=0)
                    top = newer if top is None else jnp.maximum(top, newer)
                m_ref[n] = top

    def finish(u):
        c, _, t = split(u)
        number, lent = task_of(t)

        @pl.when(lent == 0)
        def _():
            o_ref[number, :, cols(c)] = flat[...].T

        @pl.when(first & (t == 0))
        def _():
            o_ref[0, :, cols(c)] = flat[...].T
            o_ref[1, :, cols(c)] = flat_b[...].T

        @pl.when(lent == 1)
        def _():
            o_next[:, cols(c)] = flat[...].T
            give(c).start()

    count = chunks * units

    @pl.loop(0, chunks)
    def _(c):
        @pl.loop(0, frames)
        def _(n):
            row_blocks(lambda at: put_queries(c, n, q_ref[n, at, cols(c)], at))

    receive(0)
    prepare_keys(0)
    if chunks > 1:
        begin(1)
    phase(-2, 0, (s0, m0), None, None)
    phase(-1, 1, (s1, m1), (s0, m0, p0), None)
    prepare_values(0)

    @pl.loop(0, count - 2)
    def _(u):
        c, _, _ = split(u)
        step = u - c * units
        arrival = (u + 1) // ARRIVAL_UNITS

        @pl.when((step == 0) & (c + 2 < chunks))
        def _():
            begin(c + 2)

        @pl.when((u == arrival * ARRIVAL_UNITS - 1) & (arrival < chunks))
        def _():
            receive(arrival)

        @pl.when((step == units - 2) & (c + 1 < chunks))
        def _():
            prepare_keys(c + 1)
            prepare_values(c + 1)

        @pl.when(u % 2 == 0)
        def _():
            phase(u, 0, (s0, m0), (s1, m1, p1), (p0,))

        @pl.when(u % 2 == 1)
        def _():
            phase(u, 1, (s1, m1), (s0, m0, p0), (p1,))
            finish(u)

    phase(count - 2, 0, None, (s1, m1, p1), (p0,))
    phase(count - 1, 1, None, None, (p1,))
    finish(count - 1)

    @pl.loop(0, chunks)
    def _(c):
        for i in range(2):
            swap(i, c).wait_send()

            @pl.when(sends_on)
            def _():
                anchor(i, c, False).wait_send()

            @pl.when(z > 0)
            def _():
                relay(i, c).wait_send()

        @pl.when(sends_on)
        def _():
            give(c).wait_send()

        @pl.when(z > 0)
        def _():
            lend(c).wait_send()
            give(c).wait_recv()
            o_ref[0, :, cols(c)] = o_first[:, cols(c)]


def shifted(blocks, queries, key_states, value_states):
    frames, rows, columns = queries.shape
    tokens = 2 * rows
    chunks = columns // LANES
    held = pltpu.VMEM((frames + 1, tokens, columns), BF)
    flat = pltpu.VMEM((rows, columns), BF)
    dma = pltpu.SemaphoreType.DMA
    pair, single = dma((2, chunks)), dma((chunks,))
    anywhere = pl.BlockSpec(memory_space=pl.ANY)
    near = pl.BlockSpec(memory_space=pltpu.VMEM)
    scores = pltpu.VMEM((2 * tokens, rows), F32)
    weights = pltpu.VMEM((2 * tokens, rows), BF)
    tops = pltpu.VMEM((2, 8, rows), F32)
    turned_out = pltpu.VMEM((LANES, rows), BF)
    return pl.pallas_call(
        functools.partial(shifted_kernel, blocks),
        out_shape=jax.ShapeDtypeStruct(queries.shape, queries.dtype),
        in_specs=[near, anywhere, anywhere],
        out_specs=near,
        scratch_shapes=[
            held,
            held,
            flat,
            flat,
            flat,
            pltpu.VMEM((2, frames + 1, 2, HEAD_DIM + ONES_ROWS, tokens), BF),
            pltpu.VMEM((chunks, frames + 1, 2, rows, 2 * LANES), BF),
            scores,
            scores,
            weights,
            weights,
            tops,
            tops,
            turned_out,
            turned_out,
            *[pair] * 7,
            *[single] * 4,
        ],
        compiler_params=pltpu.CompilerParams(
            collective_id=0, has_side_effects=True, vmem_limit_bytes=58 * 1024 * 1024
        ),
    )(queries, key_states, value_states)


def solution(mesh):
    spec = P(("groups", "frame"), "seq", "head")
    blocks, halves = mesh.shape["frame"], mesh.shape["seq"]

    def body(queries, key_states, value_states):
        frames, rows, columns = queries.shape
        fits = columns % LANES == 0 and rows % SLOT_KEYS == 0
        if blocks > 1 and halves == 2 and frames == 4 and columns <= 640 and fits:
            return shifted(blocks, queries, key_states, value_states)
        return local(blocks, halves, queries, key_states, value_states)

    return jax.shard_map(
        body, mesh=mesh, in_specs=(spec, spec, spec), out_specs=spec, check_vma=False
    )
```

```python
import functools

import jax
import jax.numpy as jnp
from jax import lax
from jax.experimental import pallas as pl
from jax.experimental.pallas import tpu as pltpu
from jax.sharding import PartitionSpec as P

HEAD_DIM = 64
LANES = 128
KEY_BLOCK = 512


def attend_columns(q, keys, values):
    rows, width = q.shape
    heads = width // HEAD_DIM
    head_of_lane = lax.broadcasted_iota(jnp.int32, q.shape, 1) // HEAD_DIM
    scaled = q * jnp.asarray(HEAD_DIM**-0.5, q.dtype)
    stacked = jnp.concatenate(
        [jnp.where(head_of_lane == h, scaled, jnp.zeros_like(scaled)) for h in range(heads)], 0
    )
    row_max = total = None
    for k, v in zip(keys, values):
        for start in range(0, k.shape[0], KEY_BLOCK):
            k_part, v_part = k[start : start + KEY_BLOCK], v[start : start + KEY_BLOCK]
            summed = jnp.concatenate([v_part, jnp.ones_like(v_part)], 1)
            scores = lax.dot_general(
                stacked, k_part, (((1,), (1,)), ((), ())), preferred_element_type=jnp.float32
            )
            newer = jnp.max(scores, axis=1, keepdims=True)
            if row_max is not None:
                newer = jnp.maximum(row_max, newer)
            rounded = jnp.exp(scores - newer).astype(jnp.bfloat16)
            part = jnp.dot(rounded, summed, preferred_element_type=jnp.float32)
            total = part if row_max is None else total * jnp.exp(row_max - newer) + part
            row_max = newer
    out = total[:, :width] / total[:, width:]
    result = out[:rows]
    for h in range(1, heads):
        result = jnp.where(head_of_lane == h, out[h * rows : (h + 1) * rows], result)
    return result.astype(jnp.bfloat16)


def kernel(
    blocks,
    halves,
    q_ref,
    k_ref,
    v_ref,
    o_ref,
    k_buf,
    v_buf,
    own_sem,
    swap_send,
    swap_recv,
    prior_send,
    prior_recv,
    anchor_send,
    anchor_recv,
    relay_send,
    relay_recv,
):
    frames, rows, columns = q_ref.shape
    chunks = own_sem.shape[1]
    width = columns // chunks
    anchor_slot, prior_slot = frames, frames + 1
    z = lax.axis_index("frame")
    half = lax.axis_index("seq")
    later = (z + blocks - 1) // blocks
    ahead = {"frame": (z + 1) % blocks}
    first = z == 0
    sends_on = z < blocks - 1
    mine = pl.ds(pl.multiple_of(half * rows, rows), rows)
    sources, buffers = (k_ref, v_ref), (k_buf, v_buf)
    offsets = range(1, halves)

    def cols(c):
        return pl.ds(pl.multiple_of(c * width, LANES), width) if chunks > 1 else pl.ds(0, width)

    def sibling(j):
        return {"seq": (half + j) % halves}

    def remote(src, dst, send, recv, where):
        return pltpu.make_async_remote_copy(
            src_ref=src,
            dst_ref=dst,
            send_sem=send,
            recv_sem=recv,
            device_id=where,
            device_id_type=pl.DeviceIdType.MESH,
        )

    def own(i, c):
        return pltpu.make_async_copy(
            sources[i].at[pl.ds(0, frames - 1), :, cols(c)],
            buffers[i].at[pl.ds(0, frames - 1), mine, cols(c)],
            own_sem.at[i, c],
        )

    def swap(i, c, j):
        return remote(
            sources[i].at[pl.ds(0, frames - 1), :, cols(c)],
            buffers[i].at[pl.ds(0, frames - 1), mine, cols(c)],
            swap_send.at[i, c, j - 1],
            swap_recv.at[i, c, j - 1],
            sibling(j),
        )

    def prior(i, c):
        return remote(
            sources[i].at[frames - 1, :, cols(c)],
            buffers[i].at[prior_slot, mine, cols(c)],
            prior_send.at[i, c],
            prior_recv.at[i, c],
            ahead,
        )

    def anchor(i, c, root):
        here = buffers[i].at[anchor_slot, mine, cols(c)]
        return remote(
            sources[i].at[0, :, cols(c)] if root else here,
            here,
            anchor_send.at[i, c],
            anchor_recv.at[i, c],
            ahead,
        )

    def relay(which, i, c, j):
        here = buffers[i].at[anchor_slot + which, mine, cols(c)]
        return remote(
            here,
            here,
            relay_send.at[which, i, c, j - 1],
            relay_recv.at[which, i, c, j - 1],
            sibling(j),
        )

    barrier = pltpu.get_barrier_semaphore()

    @pl.when(sends_on)
    def _():
        pl.semaphore_signal(
            barrier, inc=1, device_id=ahead, device_id_type=pl.DeviceIdType.MESH
        )

    @pl.when(z > 0)
    def _():
        pl.semaphore_signal(
            barrier,
            inc=1,
            device_id={"frame": (z + blocks - 1) % blocks},
            device_id_type=pl.DeviceIdType.MESH,
        )

    for j in offsets:
        pl.semaphore_signal(
            barrier, inc=1, device_id=sibling(j), device_id_type=pl.DeviceIdType.MESH
        )
    pl.semaphore_wait(barrier, later + 1 - (z + 1) // blocks + halves - 1)

    @pl.when(first & sends_on)
    def _():
        @pl.loop(0, chunks)
        def _(c):
            for i in range(2):
                anchor(i, c, True).start()
            for i in range(2):
                prior(i, c).start()

    @pl.when((z > 0) & sends_on)
    def _():
        for i in range(2):
            prior(i, 0).start()

    @pl.loop(0, chunks)
    def _(c):
        for i in range(2):
            own(i, c).start()
            for j in offsets:
                swap(i, c, j).start()

    def receive(c):
        @pl.when(z > 0)
        def _():
            for i in range(2):
                anchor(i, c, False).wait_recv()

                @pl.when(sends_on)
                def _():
                    anchor(i, c, False).start()

                for j in offsets:
                    relay(0, i, c, j).start()

            @pl.when(sends_on & (c + 1 < chunks))
            def _():
                for i in range(2):
                    prior(i, c + 1).start()

            for i in range(2):
                prior(i, c).wait_recv()
                for j in offsets:
                    relay(1, i, c, j).start()

    def complete(c):
        for i in range(2):
            own(i, c).wait()
            for j in offsets:
                swap(i, c, j).wait_recv()

        @pl.when(z > 0)
        def _():
            for i in range(2):
                for j in offsets:
                    relay(0, i, c, j).wait_recv()
                    relay(1, i, c, j).wait_recv()

    block = min(rows, 512)
    per_frame = rows // block
    steps = frames * per_frame

    def compute(c, step):
        frame = step // per_frame
        opens = (frames - frame) // frames
        before = (frame - 1) * (1 - opens) + opens * later * prior_slot
        zero = later * anchor_slot
        at_rows = pl.ds(pl.multiple_of((step % per_frame) * block, block), block)
        for start in range(0, width, LANES):
            size = min(LANES, width - start)
            if chunks > 1:
                at = cols(c)
            else:
                at = pl.ds(start, size)
            o_ref[frame, at_rows, at] = attend_columns(
                q_ref[frame, at_rows, at],
                [k_buf[zero, :, at], k_buf[before, :, at]],
                [v_buf[zero, :, at], v_buf[before, :, at]],
            )

    receive(0)

    @pl.loop(0, chunks)
    def _(c):
        complete(c)

        @pl.loop(0, steps)
        def _(step):
            @pl.when((step == steps // 2) & (c + 1 < chunks))
            def _():
                receive(c + 1)

            compute(c, step)

    @pl.loop(0, chunks)
    def _(c):
        for i in range(2):
            for j in offsets:
                swap(i, c, j).wait_send()

            @pl.when(sends_on)
            def _():
                prior(i, c).wait_send()
                anchor(i, c, False).wait_send()

            @pl.when(z > 0)
            def _():
                for j in offsets:
                    relay(0, i, c, j).wait_send()
                    relay(1, i, c, j).wait_send()


def local(blocks, halves, queries, key_states, value_states):
    frames, rows, columns = queries.shape
    chunks = columns // LANES if columns % LANES == 0 else 1
    held = pltpu.VMEM((frames + 2, rows * halves, columns), queries.dtype)
    dma = pltpu.SemaphoreType.DMA
    plain = dma((2, chunks))
    across = dma((2, chunks, halves - 1))
    relays = dma((2, 2, chunks, halves - 1))
    anywhere = pl.BlockSpec(memory_space=pl.ANY)
    near = pl.BlockSpec(memory_space=pltpu.VMEM)
    return pl.pallas_call(
        functools.partial(kernel, blocks, halves),
        out_shape=jax.ShapeDtypeStruct(queries.shape, queries.dtype),
        in_specs=[near, anywhere, anywhere],
        out_specs=near,
        scratch_shapes=[
            held,
            held,
            plain,
            across,
            across,
            plain,
            plain,
            plain,
            plain,
            relays,
            relays,
        ],
        compiler_params=pltpu.CompilerParams(
            collective_id=0, has_side_effects=True, vmem_limit_bytes=56 * 1024 * 1024
        ),
    )(queries, key_states, value_states)


SLOT_KEYS = 256
ONES_ROWS = 16
BF = jnp.bfloat16
F32 = jnp.float32
NT = (((1,), (1,)), ((), ()))
LOG2E = 1.4426950408889634


def parts_of(q):
    scaled = q.astype(F32) * (LOG2E * HEAD_DIM**-0.5)
    high = scaled.astype(BF)
    return high, (scaled - high.astype(F32)).astype(BF)


def shifted_kernel(
    blocks,
    q_ref,
    k_ref,
    v_ref,
    o_ref,
    k_buf,
    v_buf,
    q_next,
    o_next,
    o_first,
    vt,
    parts,
    s0,
    s1,
    p0,
    p1,
    m0,
    m1,
    flat,
    flat_b,
    own_sem,
    swap_send,
    swap_recv,
    anchor_send,
    anchor_recv,
    relay_send,
    relay_recv,
    q_send,
    q_recv,
    o_send,
    o_recv,
):
    frames, rows, columns = q_ref.shape
    chunks = columns // LANES
    tokens = k_buf.shape[1]
    z = lax.axis_index("frame")
    half = lax.axis_index("seq")
    later = (z + blocks - 1) // blocks
    last = (z + 1) // blocks
    ahead = {"frame": (z + 1) % blocks}
    behind = {"frame": (z + blocks - 1) % blocks}
    sibling = {"seq": 1 - half}
    first = z == 0
    sends_on = z < blocks - 1
    mine = pl.ds(pl.multiple_of(half * rows, rows), rows)
    sources, buffers = (k_ref, v_ref), (k_buf, v_buf)
    anchor_slot = frames
    zero_slot = later * anchor_slot

    def cols(c):
        return pl.ds(pl.multiple_of(c * LANES, LANES), LANES)

    def remote(src, dst, send, recv, where):
        return pltpu.make_async_remote_copy(
            src_ref=src,
            dst_ref=dst,
            send_sem=send,
            recv_sem=recv,
            device_id=where,
            device_id_type=pl.DeviceIdType.MESH,
        )

    def own(i, c):
        return pltpu.make_async_copy(
            sources[i].at[:, :, cols(c)],
            buffers[i].at[pl.ds(0, frames), mine, cols(c)],
            own_sem.at[i, c],
        )

    def swap(i, c):
        return remote(
            sources[i].at[:, :, cols(c)],
            buffers[i].at[pl.ds(0, frames), mine, cols(c)],
            swap_send.at[i, c],
            swap_recv.at[i, c],
            sibling,
        )

    def anchor(i, c, root):
        here = buffers[i].at[anchor_slot, mine, cols(c)]
        return remote(
            sources[i].at[0, :, cols(c)] if root else here,
            here,
            anchor_send.at[i, c],
            anchor_recv.at[i, c],
            ahead,
        )

    def relay(i, c):
        here = buffers[i].at[anchor_slot, mine, cols(c)]
        return remote(here, here, relay_send.at[i, c], relay_recv.at[i, c], sibling)

    def lend(c):
        return remote(
            q_ref.at[0, :, cols(c)], q_next.at[:, cols(c)], q_send.at[c], q_recv.at[c], behind
        )

    def give(c):
        return remote(
            o_next.at[:, cols(c)], o_first.at[:, cols(c)], o_send.at[c], o_recv.at[c], ahead
        )

    barrier = pltpu.get_barrier_semaphore()

    def greet(where):
        pl.semaphore_signal(barrier, inc=1, device_id=where, device_id_type=pl.DeviceIdType.MESH)

    @pl.when(sends_on)
    def _():
        greet(ahead)

    @pl.when(z > 0)
    def _():
        greet(behind)

    greet(sibling)
    pl.semaphore_wait(barrier, later + 1 - last + 1)

    def begin(c):
        for i in range(2):
            @pl.when(first & sends_on)
            def _():
                anchor(i, c, True).start()

            swap(i, c).start()
            own(i, c).start()
            if i == 0:
                @pl.when(z > 0)
                def _():
                    lend(c).start()

    begin(0)
    vt[:, :, :, HEAD_DIM:, :] = jnp.ones((*vt.shape[:3], ONES_ROWS, tokens), BF)

    def receive(c):
        @pl.when(z > 0)
        def _():
            for i in range(2):
                anchor(i, c, False).wait_recv()

                @pl.when(sends_on)
                def _():
                    anchor(i, c, False).start()

                relay(i, c).start()

    low_lanes = lax.broadcasted_iota(jnp.int32, (SLOT_KEYS, LANES), 1) < HEAD_DIM

    def landed(i, c):
        own(i, c).wait()
        swap(i, c).wait_recv()

        @pl.when(z > 0)
        def _():
            relay(i, c).wait_recv()

    def put_queries(c, n, q, at):
        for t, part in enumerate(parts_of(q)):
            lanes = pl.ds(t * LANES, LANES)
            none = jnp.zeros_like(part)
            parts[c, n, 0, at, lanes] = jnp.where(low_lanes, part, none)
            parts[c, n, 1, at, lanes] = jnp.where(low_lanes, none, part)

    def row_blocks(body):
        @pl.loop(0, rows // SLOT_KEYS)
        def _(b):
            body(pl.ds(pl.multiple_of(b * SLOT_KEYS, SLOT_KEYS), SLOT_KEYS))

    def prepare_keys(c):
        landed(0, c)

        @pl.when(sends_on)
        def _():
            lend(c).wait_recv()
            row_blocks(lambda at: put_queries(c, frames, q_next[at, cols(c)], at))

    def prepare_values(c):
        par = c % 2
        landed(1, c)

        @pl.loop(0, frames + later * (1 - last))
        def _(n):
            slot = n + last * (n // (frames - 1))

            @pl.loop(0, tokens // rows)
            def _(b):
                at = pl.ds(pl.multiple_of(b * rows, rows), rows)
                v = v_buf[slot, at, cols(c)].T
                vt[par, slot, 0, 0:HEAD_DIM, at] = v[:HEAD_DIM]
                vt[par, slot, 1, 0:HEAD_DIM, at] = v[HEAD_DIM:]

    tasks = frames - last
    units = 2 * tasks

    def flag(x):
        return jnp.where(x, 1, 0)

    def task_of(t):
        lent = (1 - last) * flag(t == frames - 2)
        final = flag(t == tasks - 1)
        return lent * frames + (1 - lent) * (t + 1 + final * (frames - 2 - t)), lent

    def split(u):
        c = sum(flag(u >= n * units) for n in range(1, chunks))
        return c, c % 2, (u - c * units) // 2

    def phase(u, head, a, b, cc):
        if b is not None:
            s_ref, m_ref, p_ref = b
            _, _, t = split(u + 1)
            joint = jnp.where(first & (t == 0), 0.0, 1.0).astype(F32)
            ma = jnp.max(m_ref[0], axis=0, keepdims=True)
            mb = jnp.max(m_ref[1], axis=0, keepdims=True)
            both = jnp.maximum(ma, mb)
            tops = [jnp.where(joint > 0.5, both, x) for x in (ma, mb)]
            for n in range(2):
                for k0 in range(n * tokens, (n + 1) * tokens, SLOT_KEYS):
                    at = slice(k0, k0 + SLOT_KEYS)
                    p_ref[at, :] = jnp.exp2(s_ref[at, :] - tops[n]).astype(BF)
        if cc is not None:
            (p_ref,) = cc
            c, par, t = split(u)
            number, lent = task_of(t)
            part_a = jnp.dot(
                vt[par, zero_slot, head], p_ref[:tokens, :], preferred_element_type=F32
            )
            part_b = jnp.dot(
                vt[par, number - 1, head], p_ref[tokens:, :], preferred_element_type=F32
            )
            alone = first & (t == 0)
            total = part_a + jnp.where(flag(alone) > 0, jnp.zeros_like(part_b), part_b)
            mine_rows = slice(head * HEAD_DIM, (head + 1) * HEAD_DIM)
            one = 1.0 / total[HEAD_DIM : HEAD_DIM + 1]
            flat[mine_rows, :] = (total[:HEAD_DIM] * one).astype(BF)
            one = 1.0 / part_b[HEAD_DIM : HEAD_DIM + 1]
            flat_b[mine_rows, :] = (part_b[:HEAD_DIM] * one).astype(BF)
        if a is not None:
            s_ref, m_ref = a
            c, _, t = split(u + 2)
            number, _ = task_of(t)
            alone = jnp.where(first & (t == 0), 1, 0)
            places = ((zero_slot, number - alone), (number - 1, number))
            for n, (slot, frame) in enumerate(places):
                q = parts[c, frame, head]
                top = None
                for k0 in range(0, tokens, SLOT_KEYS):
                    k = k_buf[slot, k0 : k0 + SLOT_KEYS, cols(c)]
                    scores = lax.dot_general(
                        jnp.concatenate([k, k], 1), q, NT, preferred_element_type=F32
                    )
                    s_ref[n * tokens + k0 : n * tokens + k0 + SLOT_KEYS, :] = scores
                    newer = jnp.max(scores.reshape(SLOT_KEYS // 8, 8, rows), axis=0)
                    top = newer if top is None else jnp.maximum(top, newer)
                m_ref[n] = top

    def finish(u):
        c, _, t = split(u)
        number, lent = task_of(t)

        @pl.when(lent == 0)
        def _():
            o_ref[number, :, cols(c)] = flat[...].T

        @pl.when(first & (t == 0))
        def _():
            o_ref[0, :, cols(c)] = flat[...].T
            o_ref[1, :, cols(c)] = flat_b[...].T

        @pl.when(lent == 1)
        def _():
            o_next[:, cols(c)] = flat[...].T
            give(c).start()

    count = chunks * units

    @pl.loop(0, chunks)
    def _(c):
        @pl.loop(0, frames)
        def _(n):
            row_blocks(lambda at: put_queries(c, n, q_ref[n, at, cols(c)], at))

    receive(0)
    prepare_keys(0)
    if chunks > 1:
        begin(1)
    phase(-2, 0, (s0, m0), None, None)
    phase(-1, 1, (s1, m1), (s0, m0, p0), None)
    prepare_values(0)

    @pl.loop(0, count - 2)
    def _(u):
        c, _, _ = split(u)
        step = u - c * units

        @pl.when((step == 0) & (c + 2 < chunks))
        def _():
            begin(c + 2)

        @pl.when((step == units - 6) & (c + 1 < chunks))
        def _():
            receive(c + 1)

        @pl.when((step == units - 2) & (c + 1 < chunks))
        def _():
            prepare_keys(c + 1)
            prepare_values(c + 1)

        @pl.when(u % 2 == 0)
        def _():
            phase(u, 0, (s0, m0), (s1, m1, p1), (p0,))

        @pl.when(u % 2 == 1)
        def _():
            phase(u, 1, (s1, m1), (s0, m0, p0), (p1,))
            finish(u)

    phase(count - 2, 0, None, (s1, m1, p1), (p0,))
    phase(count - 1, 1, None, None, (p1,))
    finish(count - 1)

    @pl.loop(0, chunks)
    def _(c):
        for i in range(2):
            swap(i, c).wait_send()

            @pl.when(sends_on)
            def _():
                anchor(i, c, False).wait_send()

            @pl.when(z > 0)
            def _():
                relay(i, c).wait_send()

        @pl.when(sends_on)
        def _():
            give(c).wait_send()

        @pl.when(z > 0)
        def _():
            lend(c).wait_send()
            give(c).wait_recv()
            o_ref[0, :, cols(c)] = o_first[:, cols(c)]


def shifted(blocks, queries, key_states, value_states):
    frames, rows, columns = queries.shape
    tokens = 2 * rows
    chunks = columns // LANES
    held = pltpu.VMEM((frames + 1, tokens, columns), BF)
    flat = pltpu.VMEM((rows, columns), BF)
    dma = pltpu.SemaphoreType.DMA
    pair, single = dma((2, chunks)), dma((chunks,))
    anywhere = pl.BlockSpec(memory_space=pl.ANY)
    near = pl.BlockSpec(memory_space=pltpu.VMEM)
    scores = pltpu.VMEM((2 * tokens, rows), F32)
    weights = pltpu.VMEM((2 * tokens, rows), BF)
    tops = pltpu.VMEM((2, 8, rows), F32)
    turned_out = pltpu.VMEM((LANES, rows), BF)
    return pl.pallas_call(
        functools.partial(shifted_kernel, blocks),
        out_shape=jax.ShapeDtypeStruct(queries.shape, queries.dtype),
        in_specs=[near, anywhere, anywhere],
        out_specs=near,
        scratch_shapes=[
            held,
            held,
            flat,
            flat,
            flat,
            pltpu.VMEM((2, frames + 1, 2, HEAD_DIM + ONES_ROWS, tokens), BF),
            pltpu.VMEM((chunks, frames + 1, 2, rows, 2 * LANES), BF),
            scores,
            scores,
            weights,
            weights,
            tops,
            tops,
            turned_out,
            turned_out,
            *[pair] * 7,
            *[single] * 4,
        ],
        compiler_params=pltpu.CompilerParams(
            collective_id=0, has_side_effects=True, vmem_limit_bytes=58 * 1024 * 1024
        ),
    )(queries, key_states, value_states)


def solution(mesh):
    spec = P(("groups", "frame"), "seq", "head")
    blocks, halves = mesh.shape["frame"], mesh.shape["seq"]

    def body(queries, key_states, value_states):
        frames, rows, columns = queries.shape
        fits = columns % LANES == 0 and rows % SLOT_KEYS == 0
        if blocks > 1 and halves == 2 and frames == 4 and columns <= 640 and fits:
            return shifted(blocks, queries, key_states, value_states)
        return local(blocks, halves, queries, key_states, value_states)

    return jax.shard_map(
        body, mesh=mesh, in_specs=(spec, spec, spec), out_specs=spec, check_vma=False
    )
```
